32 devices in a mesh: group: 2 (over y), ctx: 4 (over z), head: 4 (over x, core).
Axes of the slice: x: 2, y: 2, z: 4, core: 2. Of those that a mesh axis runs over, the one named last changes fastest.
Arguments:
- mixer_x: bfloat16 [2048, 8192], P(('group', 'ctx'), 'head'), parts along dimension 0, may hold values from -6 to 6
- mixer_bc: bfloat16 [2, 2048, 1024], P(None, ('group', 'ctx'), 'head'), parts along dimension 1, may hold values from -3 to 3
- mixer_gate: bfloat16 [2048, 8192], P(('group', 'ctx'), 'head'), parts along dimension 0, may hold values from -9 to 9
- step_logits: float32 [2048, 128], P(('group', 'ctx'), 'head'), parts along dimension 0, may hold values from -3 to 3
- conv_x_weight: float32 [4, 8192], P(None, 'head'), may hold values from -0.6 to 0.6
- conv_bc_weight: float32 [2, 4, 1024], P(None, None, 'head'), may hold values from -0.6 to 0.6
- head_params: float32 [3, 128], P(None, 'head'), as said below
- norm_gain: float32 [8192], P('head'), may hold values from 0.5 to 1.5
- grad_output: bfloat16 [2048, 8192], P(('group', 'ctx'), 'head'), parts along dimension 0, may hold values from -9 to 9
Outputs:
- grad_x: bfloat16 [2048, 8192], P(('group', 'ctx'), 'head'), parts along dimension 0
- grad_bc: bfloat16 [2, 2048, 1024], P(None, ('group', 'ctx'), 'head'), parts along dimension 1
- grad_gate: bfloat16 [2048, 8192], P(('group', 'ctx'), 'head'), parts along dimension 0
- grad_step: float32 [2048, 128], P(('group', 'ctx'), 'head'), parts along dimension 0
- grad_conv_x: float32 [8, 8192], P('group', 'head'), parts along dimension 0
- grad_conv_bc: float32 [4, 4, 1024], P('group', None, 'head'), parts along dimension 0
- grad_heads: float32 [6, 128], P('group', 'head'), parts along dimension 0
- grad_gain: float32 [16384], P(('group', 'head')), parts along dimension 0
The draws below stay inside these ranges and needn't reach their ends.
There are 2 independent parts, one for each index of `group`. The reference program is written for one: setup_inputs(seed, part) draws one part's arguments, and reference() takes and returns one part's arrays. A program takes and returns all parts, laid end to end along the dimension named above; an argument that names none is the same for every part. Nothing has to cross between parts.
Inputs may be any that keep to these rules, and one draw needn't show every extreme that they name: `head_params`: row 0 is added to the step logits and lies between -1 and 1; row 1 is the logarithm of a decay rate between log(0.2 / 1024) and log(0.1); row 2 is a skip factor between 0.5 and 1.5.
All inputs are finite; a program needn't handle non-finite values.
Results may differ from the reference program's by a relative error of at most 0.014.
Values may be sent and summed in bfloat16 or wider, within the bound.
A program may use at most 128 MiB of HBM per device.

```python
import math
import jax
import jax.numpy as jnp
from jax import lax

HEADS = 128
HEAD_DIM = 64
STATE = 128
GROUPS = 8
CONV = 4
SPAN = 256
INNER = 8192
LENGTH = 1024


def draw_mixer_gate(key, part):
    column = jnp.arange(INNER, dtype=jnp.float32) / INNER
    values = jnp.clip(jax.random.normal(key, (LENGTH, INNER), jnp.float32), -5.0, 5.0)
    ramp = 0.6 + 1.2 * column
    return (values * ramp[None, :]).astype(jnp.bfloat16)


def draw_grad_output(key, part):
    row = jnp.arange(LENGTH, dtype=jnp.float32) / LENGTH
    values = jnp.clip(jax.random.normal(key, (LENGTH, INNER), jnp.float32), -5.0, 5.0)
    ramp = 0.5 + row
    return (values * ramp[:, None]).astype(jnp.bfloat16)


def draw_head_params(key, part):
    keys = jax.random.split(key, 5)
    bias = jax.random.uniform(keys[0], (HEADS,), jnp.float32, -1.0, 1.0)
    share = 0.5
    picker = jax.random.uniform(keys[1], (HEADS,), jnp.float32, 0.0, 1.0)
    quick = jnp.exp(jax.random.uniform(keys[2], (HEADS,), jnp.float32, math.log(0.025), math.log(0.1)))
    slow = jnp.exp(jax.random.uniform(keys[3], (HEADS,), jnp.float32, math.log(0.2), math.log(2.0))) / LENGTH
    log_rate = jnp.log(jnp.where(picker < share, quick, slow))
    skip_gain = jax.random.uniform(keys[4], (HEADS,), jnp.float32, 0.5, 1.5)
    return jnp.stack([bias, log_rate, skip_gain])


def steps_of(key, shape, shards, least, top_value):
    def one(dim, shards_of):
        draws = jax.random.uniform(jax.random.fold_in(jax.random.fold_in(key, 6), dim), (shards_of,), jnp.float32, least / len(shards), top_value / len(shards))
        return jnp.repeat(jnp.exp(draws), shape[dim] // shards_of).reshape((-1,) + (1,) * (len(shape) - dim - 1))

    gain = one(*shards[0])
    for cut in shards[1:]:
        gain = gain * one(*cut)
    return gain


def normal_values(stream_key, dims, width, limit, cuts=(), kind=jnp.bfloat16):
    result = jax.random.normal(stream_key, dims, jnp.float32) * width
    if len(cuts) > 0:
        result = steps_of(stream_key, dims, cuts, -0.22, 0.18) * result
    return jnp.clip(result, min=-limit, max=limit).astype(kind)


def setup_inputs(seed: int = 0, part: int = 0) -> dict:
    splits = jax.random.split(jax.random.key(seed), 10)
    own_keys = jax.random.split(jax.random.fold_in(splits[9], part), 10)
    return {
        "mixer_x": normal_values(own_keys[0], (LENGTH, INNER), 1.0, 6.0, ((0, 4), (1, 4))),
        "mixer_bc": normal_values(own_keys[1], (2, LENGTH, GROUPS * STATE), 0.5, 3.0, ((1, 4), (2, 4))),
        "mixer_gate": draw_mixer_gate(jax.random.fold_in(jax.random.fold_in(splits[9], part), 71), part),
        "step_logits": normal_values(own_keys[3], (LENGTH, HEADS), 0.5, 3.0, ((0, 4), (1, 4)), jnp.float32),
        "conv_x_weight": jnp.clip(jax.random.uniform(splits[4], (CONV, INNER), jnp.float32, -0.6, 0.6) * steps_of(splits[4], (CONV, INNER), ((1, 4),), -0.4, 0.0), -0.6, 0.6),
        "conv_bc_weight": jnp.clip(jax.random.uniform(splits[5], (2, CONV, GROUPS * STATE), jnp.float32, -0.6, 0.6) * steps_of(splits[5], (2, CONV, GROUPS * STATE), ((2, 4),), -0.4, 0.0), -0.6, 0.6),
        "head_params": draw_head_params(jax.random.fold_in(splits[9], 71), part),
        "norm_gain": jnp.clip(1.0 + 0.1 * jax.random.normal(splits[7], (INNER,), jnp.float32), 0.5, 1.5),
        "grad_output": draw_grad_output(jax.random.fold_in(jax.random.fold_in(splits[9], part), 71), part),
    }


epsilon = 1e-05

def conv_silu(padded_rows, kernel):
    taps_count = kernel.shape[0]
    out_rows = padded_rows.shape[0] - taps_count + 1
    summed = kernel[0] * padded_rows[0:out_rows]
    for offset in range(1, taps_count):
        summed = summed + kernel[offset] * padded_rows[offset:offset + out_rows]
    return jax.nn.silu(summed).astype(jnp.bfloat16)

def span_parts(x_block, b_block, c_block, step_block, decay_rate, skip_gain):
    log_decay = jnp.cumsum(step_block * decay_rate, axis=0)
    block_end = log_decay[-1]
    scores = jnp.einsum('tgn,sgn->gts', c_block, b_block, preferred_element_type=jnp.float32)
    by_head = jnp.transpose(log_decay, (1, 2, 0))
    spread = by_head[:, :, :, None] - by_head[:, :, None, :]
    positions = jnp.arange(log_decay.shape[0])
    causal = positions[:, None] >= positions[None, :]
    weights = jnp.where(causal, jnp.exp(jnp.where(causal, spread, 0.0)), 0.0)
    step_heads = jnp.transpose(step_block, (1, 2, 0))
    mixing = (scores[:, None] * weights * step_heads[:, :, None, :]).astype(jnp.bfloat16)
    inside = jnp.einsum('gkts,sgkp->tgkp', mixing, x_block, preferred_element_type=jnp.float32)
    inside = inside + skip_gain[None, :, :, None] * x_block.astype(jnp.float32)
    carry_weight = jnp.exp(block_end[None] - log_decay) * step_block
    scaled_x = (x_block.astype(jnp.float32) * carry_weight[..., None]).astype(jnp.bfloat16)
    block_state = jnp.einsum('sgkp,sgn->gkpn', scaled_x, b_block, preferred_element_type=jnp.float32)
    return (inside, block_state, block_end, log_decay)

def state_read(c_block, state_low, log_decay):
    readout = jnp.einsum('tgn,gkpn->tgkp', c_block, state_low, preferred_element_type=jnp.float32)
    return readout * jnp.exp(log_decay)[..., None]

def forward(mixer_x, mixer_bc, mixer_gate, step_logits, conv_x_weight, conv_bc_weight, head_params, norm_gain):
    margin = CONV - 1
    per_group = HEADS // GROUPS
    blocks = LENGTH // SPAN
    x_conv = conv_silu(jnp.pad(mixer_x.astype(jnp.float32), ((margin, 0), (0, 0))), conv_x_weight)
    b_conv = conv_silu(jnp.pad(mixer_bc[0].astype(jnp.float32), ((margin, 0), (0, 0))), conv_bc_weight[0])
    c_conv = conv_silu(jnp.pad(mixer_bc[1].astype(jnp.float32), ((margin, 0), (0, 0))), conv_bc_weight[1])
    step_size = jax.nn.softplus(step_logits + head_params[0])
    decay_rate = (-jnp.exp(head_params[1])).reshape(GROUPS, per_group)
    skip_gain = head_params[2].reshape(GROUPS, per_group)
    x_blocks = x_conv.reshape(blocks, SPAN, GROUPS, per_group, HEAD_DIM)
    b_blocks = b_conv.reshape(blocks, SPAN, GROUPS, STATE)
    c_blocks = c_conv.reshape(blocks, SPAN, GROUPS, STATE)
    step_blocks = step_size.reshape(blocks, SPAN, GROUPS, per_group)

    def advance(carried, pieces):
        x_block, b_block, c_block, step_block = pieces
        inside, block_state, block_end, log_decay = span_parts(x_block, b_block, c_block, step_block, decay_rate, skip_gain)
        output = inside + state_read(c_block, carried.astype(jnp.bfloat16), log_decay)
        carried = jnp.exp(block_end)[..., None, None] * carried + block_state
        return (carried, output)
    initial = jnp.zeros((GROUPS, per_group, HEAD_DIM, STATE), jnp.float32)
    _, outputs = lax.scan(jax.checkpoint(advance), initial, (x_blocks, b_blocks, c_blocks, step_blocks))
    mixed = outputs.reshape(LENGTH, INNER)
    gate_value = mixer_gate.astype(jnp.float32)
    gated = mixed * (gate_value * jax.nn.sigmoid(gate_value))
    factor = lax.rsqrt(lax.optimization_barrier(jnp.sum(gated * gated, axis=1)) / INNER + epsilon)
    return gated * factor[:, None] * norm_gain

def reference(mixer_x, mixer_bc, mixer_gate, step_logits, conv_x_weight, conv_bc_weight, head_params, norm_gain, grad_output):
    _, pull_back = jax.vjp(forward, mixer_x, mixer_bc, mixer_gate, step_logits, conv_x_weight, conv_bc_weight, head_params, norm_gain)
    gradients = pull_back(grad_output.astype(jnp.float32))
    return (gradients[0].astype(jnp.bfloat16), gradients[1].astype(jnp.bfloat16), gradients[2].astype(jnp.bfloat16), gradients[3], gradients[4], gradients[5], gradients[6], gradients[7])
```

```python
import functools

import jax
import jax.numpy as jnp
from jax import lax
from jax.experimental import pallas as pl
from jax.experimental.pallas import tpu as pltpu
from jax.sharding import PartitionSpec as P

HEADS = 128
HEAD_DIM = 64
STATE = 128
GROUPS = 8
CONV = 4
SPAN = 256
INNER = 8192
PER_GROUP = HEADS // GROUPS
CHUNK = 256
HPC = CHUNK // HEAD_DIM
LOW = -1e30
epsilon = 1e-05

F32 = jnp.float32
BF16 = jnp.bfloat16
MESH = pl.DeviceIdType.MESH
HIGH = lax.Precision.HIGHEST


def dot(a, b, ca=1, cb=0, precision=None):
    return lax.dot_general(
        a, b, (((ca,), (cb,)), ((), ())), precision=precision, preferred_element_type=F32
    )


def sigmoid(v):
    return 1.0 / (1.0 + jnp.exp(-v))


def split_dot(a, sel):
    high = a.astype(BF16)
    low = (a - high.astype(F32)).astype(BF16)
    return dot(high, sel) + dot(low, sel)


def kernel(
    n_ctx, n_head,
    x_ref, bc_ref, gate_ref, logits_ref, wx_ref, wbc_ref, params_ref, gain_ref, go_ref,
    gx_ref, gbc_ref, ggate_ref, gstep_ref, gwx_ref, gwbc_ref, gparams_ref, ggain_ref,
    halo_x, halo_bc, cum_b, cum_p, step_p, cum_t, step_t, mask, tap, dtap,
    xc, pre_x, bcc, pre_bc, b_t, c_t, scores, mix, weight, scaled, added,
    f_recv, f_send, r_recv, r_send, mixed, d_mixed, acc_sq, acc_proj, stats,
    d_b, d_c, d_s, acc1, acc2, acc_row, border_send, border_recv, tail_x, tail_bc,
    part, totals,
    halo_s, halo_r, f_ss, f_rs, r_ss, r_rs, st_s, st_r, bo_s, bo_r, to_s, to_r,
):
    me = lax.axis_index("ctx")
    mh = lax.axis_index("head")
    T = x_ref.shape[0]
    width = x_ref.shape[1]
    columns = bc_ref.shape[2]
    groups = columns // STATE
    heads = width // HEAD_DIM
    chunks = width // CHUNK
    per_g = chunks // groups
    nxt = lax.rem(me + 1, n_ctx)
    prv = lax.rem(me + n_ctx - 1, n_ctx)

    barrier = pltpu.get_barrier_semaphore()
    for k in range(1, n_ctx):
        pl.semaphore_signal(
            barrier, inc=1, device_id={"ctx": lax.rem(me + k, n_ctx)}, device_id_type=MESH
        )
    for k in range(1, n_head):
        pl.semaphore_signal(
            barrier, inc=1, device_id={"head": lax.rem(mh + k, n_head)}, device_id_type=MESH
        )
    pl.semaphore_wait(barrier, n_ctx - 1 + n_head - 1)

    def remote(src, dst, s, r, **where):
        return pltpu.make_async_remote_copy(
            src_ref=src, dst_ref=dst, send_sem=s, recv_sem=r, device_id=where, device_id_type=MESH
        )

    halo_copies = [
        remote(x_ref.at[pl.ds(T - 16, 16), :], halo_x, halo_s.at[0], halo_r.at[0], ctx=nxt),
        remote(bc_ref.at[:, pl.ds(T - 16, 16), :], halo_bc, halo_s.at[1], halo_r.at[1], ctx=nxt),
    ]

    @pl.when(me < n_ctx - 1)
    def _():
        for c in halo_copies:
            c.start()

    shifted = logits_ref[...] + params_ref[0:1, :]
    step = jnp.maximum(shifted, 0.0) + jnp.log1p(jnp.exp(-jnp.abs(shifted)))
    rate = -jnp.exp(params_ref[1:2, :])
    rows = lax.broadcasted_iota(jnp.int32, (T, T), 0)
    cols = lax.broadcasted_iota(jnp.int32, (T, T), 1)
    lower = jnp.where(rows >= cols, 1.0, 0.0)
    mask[...] = jnp.where(rows >= cols, 0.0, LOW)
    cum = dot(lower, step * rate, precision=HIGH)
    cum_t[...] = jnp.transpose(cum)
    step_t[...] = jnp.transpose(step)
    half = lax.broadcasted_iota(jnp.int32, (T, 128), 1) < HEAD_DIM
    for h in range(heads):
        cum_b[h] = jnp.broadcast_to(cum[:, h : h + 1], (T, 128))
    for h in range(0, heads, 2):
        pair = slice((h // 2 % 2) * 128, (h // 2 % 2) * 128 + 128)
        cum_p[h // 4, :, pair] = jnp.where(half, cum_b[h], cum_b[h + 1])
        step_p[h // 4, :, pair] = jnp.where(
            half,
            jnp.broadcast_to(step[:, h : h + 1], (T, 128)),
            jnp.broadcast_to(step[:, h + 1 : h + 2], (T, 128)),
        )

    @pl.when(me > 0)
    def _():
        for c in halo_copies:
            c.wait_recv()

    @pl.when(me == 0)
    def _():
        halo_x[...] = jnp.zeros_like(halo_x)
        halo_bc[...] = jnp.zeros_like(halo_bc)

    @pl.when(me < n_ctx - 1)
    def _():
        for c in halo_copies:
            c.wait_send()

    def convolve(lanes, w):
        total = w[0:1] * tap[pl.ds(5, T), 0:lanes]
        for k in range(1, CONV):
            total = total + w[k : k + 1] * tap[pl.ds(5 + k, T), 0:lanes]
        return total

    for kind in range(2):
        for g in range(groups):
            at = slice(g * STATE, (g + 1) * STATE)
            tap[0:8, 0:STATE] = halo_bc[kind, :, at].astype(F32)[8:16]
            tap[8 : 8 + T, 0:STATE] = bc_ref[kind, :, at].astype(F32)
            pre = convolve(STATE, wbc_ref[kind, :, at])
            pre_bc[kind, g] = pre
            bcc[kind, g] = (pre * sigmoid(pre)).astype(BF16)
    for g in range(groups):
        b_t[g] = jnp.transpose(bcc[0, g].astype(F32)).astype(BF16)
        c_t[g] = jnp.transpose(bcc[1, g].astype(F32)).astype(BF16)
        scores[g] = dot(bcc[1, g], b_t[g])
        d_b[g] = jnp.zeros((T, STATE), F32)
        d_c[g] = jnp.zeros((T, STATE), F32)
        d_s[g] = jnp.zeros((T, T), F32)
    acc_sq[...] = jnp.zeros_like(acc_sq)
    acc_proj[...] = jnp.zeros_like(acc_proj)
    acc1[...] = jnp.zeros_like(acc1)
    acc2[...] = jnp.zeros_like(acc2)
    acc_row[...] = jnp.zeros_like(acc_row)
    part[...] = jnp.zeros_like(part)

    def span(c):
        return pl.ds(pl.multiple_of(c * CHUNK, CHUNK), CHUNK)

    sel_row = lax.broadcasted_iota(jnp.int32, (CHUNK, heads), 0) // HEAD_DIM
    sel_col = lax.broadcasted_iota(jnp.int32, (CHUNK, heads), 1)

    def selector(c):
        return jnp.where(sel_row + c * HPC == sel_col, 1.0, 0.0)

    def expand(c):
        return dot(params_ref[...], selector(c), ca=1, cb=1, precision=HIGH)[2:3]

    def forward_copy(c):
        return remote(f_send.at[c], f_recv.at[c], f_ss.at[c], f_rs.at[c], ctx=nxt)

    def reverse_copy(c):
        return remote(r_send.at[c], r_recv.at[c], r_ss.at[c], r_rs.at[c], ctx=prv)

    def prepare(c, carry):
        at = span(c)
        tap[0:8, :] = halo_x[:, at].astype(F32)[8:16]
        tap[8 : 8 + T, :] = x_ref[:, at].astype(F32)
        pre = convolve(CHUNK, wx_ref[:, at])
        pre_x[:, at] = pre
        x_low = (pre * sigmoid(pre)).astype(BF16)
        xc[:, at] = x_low
        cum_c = cum_p[c]
        carry_weight = jnp.exp(cum_c[T - 1 : T] - cum_c) * step_p[c]
        sc = (x_low.astype(F32) * carry_weight).astype(BF16)
        scaled[:, at] = sc
        added[:, at] = dot(b_t[c // per_g], sc)
        return carry

    def head_loop_forward(c):
        g = c // per_g
        base = scores[g]
        out = []
        for pair in range(HPC // 2):
            x_pair = xc[:, pl.ds(pl.multiple_of(c * CHUNK + pair * 128, 128), 128)]
            ys = []
            for q in range(2):
                h = c * HPC + pair * 2 + q
                col = cum_b[h]
                spread = jnp.concatenate([col, col], axis=1) - cum_t[pl.ds(h, 1), :] + mask[...]
                w = jnp.exp(spread) * step_t[pl.ds(h, 1), :]
                weight[h] = w
                m = (base * w).astype(BF16)
                mix[h] = m
                ys.append(dot(m, x_pair))
            out.append(jnp.where(half, ys[0], ys[1]))
        return jnp.concatenate(out, axis=1)

    def forward(c, carry):
        at = span(c)
        g = c // per_g
        prepare(c, 0)
        inside = head_loop_forward(c)
        cum_c = cum_p[c]

        @pl.when(me > 0)
        def _():
            forward_copy(c).wait_recv()

        @pl.when(me == 0)
        def _():
            f_recv[c] = jnp.zeros((STATE, CHUNK), BF16)

        held = f_recv[c]
        decay = jnp.exp(cum_c[T - 1 : T])
        f_send[c] = (decay * held.astype(F32) + added[:, at]).astype(BF16)

        @pl.when(me < n_ctx - 1)
        def _():
            forward_copy(c).start()

        readout = dot(bcc[1, g], held)
        own = inside + jnp.exp(cum_c) * readout
        x_f = xc[:, at].astype(F32)
        total = own + expand(c) * x_f
        mixed[:, at] = total
        gate = gate_ref[:, at].astype(F32)
        gated = total * (gate * sigmoid(gate))
        upstream = go_ref[:, at].astype(F32) * gain_ref[:, at]
        acc_sq[...] += gated * gated
        acc_proj[...] += upstream * gated
        return carry

    lax.fori_loop(0, chunks, forward, 0)

    ones = jnp.ones((8, CHUNK), F32)
    stats[mh, 0:8, :] = dot(ones, acc_sq[...], ca=1, cb=1, precision=HIGH)
    stats[mh, 8:16, :] = dot(ones, acc_proj[...], ca=1, cb=1, precision=HIGH)

    def stat_copy(k):
        return remote(
            stats.at[mh], stats.at[mh], st_s.at[k], st_r.at[k], head=lax.rem(mh + k, n_head)
        )

    for k in range(1, n_head):
        stat_copy(k).start()
    for k in range(1, n_head):
        source = lax.rem(mh + n_head - k, n_head)
        remote(stats.at[source], stats.at[source], st_s.at[k], st_r.at[k], head=source).wait_recv()
    for k in range(1, n_head):
        stat_copy(k).wait_send()
    total_stats = stats[0]
    for k in range(1, n_head):
        total_stats = total_stats + stats[k]
    eighth = jnp.full((8, CHUNK), 0.125, F32)
    square = dot(total_stats[0:8], eighth, ca=0, cb=0, precision=HIGH)
    raw_proj = dot(total_stats[8:16], eighth, ca=0, cb=0, precision=HIGH)
    factor = lax.rsqrt(square / INNER + epsilon)
    acc_sq[...] = factor
    acc_proj[...] = raw_proj * factor / INNER

    dtap[0:8, :] = jnp.zeros((8, CHUNK), F32)
    dtap[8 + T : 16 + T, :] = jnp.zeros((8, CHUNK), F32)

    def conv_back(lanes, d_pre, w):
        dtap[8 : 8 + T, 0:lanes] = d_pre
        total = w[0:1] * dtap[pl.ds(3, T + 8), 0:lanes]
        for k in range(1, CONV):
            total = total + w[k : k + 1] * dtap[pl.ds(3 - k, T + 8), 0:lanes]
        taps = [
            jnp.sum(d_pre * tap[pl.ds(5 + k, T), 0:lanes], axis=0, keepdims=True)
            for k in range(CONV)
        ]
        return total, taps

    def silu_slope(v):
        s = sigmoid(v)
        return s * (1.0 + v * (1.0 - s))

    def gate_back(c, carry):
        at = span(c)
        g = c // per_g
        total = mixed[:, at]
        gate = gate_ref[:, at].astype(F32)
        sig = sigmoid(gate)
        act = gate * sig
        factor_c = acc_sq[...]
        go = go_ref[:, at].astype(F32)
        normed = total * act * factor_c
        d_gated = (go * gain_ref[:, at] - normed * acc_proj[...]) * factor_c
        part[4:5, at] = jnp.sum(go * normed, axis=0, keepdims=True)
        ggate_ref[:, at] = (d_gated * total * (sig * (1.0 + gate * (1.0 - sig)))).astype(BF16)
        dy = d_gated * act
        d_mixed[:, at] = dy
        cum_c = cum_p[c]
        dye = (dy * jnp.exp(cum_c)).astype(BF16)
        d_enter = dot(c_t[g], dye).astype(BF16).astype(F32)

        @pl.when(me < n_ctx - 1)
        def _():
            reverse_copy(c).wait_recv()

        @pl.when(me == n_ctx - 1)
        def _():
            r_recv[c] = jnp.zeros((STATE, CHUNK), BF16)

        after = r_recv[c]
        after_f = after.astype(F32)
        decay = jnp.exp(cum_c[T - 1 : T])
        r_send[c] = (d_enter + decay * after_f).astype(BF16)

        @pl.when(me > 0)
        def _():
            reverse_copy(c).start()

        held = f_recv[c]
        d_c[g] += dot(dye, held, ca=1, cb=1)
        x_low = xc[:, at]
        x_f = x_low.astype(F32)
        d_scaled = dot(bcc[0, g], after).astype(BF16).astype(F32)
        d_b[g] += dot(scaled[:, at], after, ca=1, cb=1)
        d_w = d_scaled * jnp.exp(cum_c[T - 1 : T] - cum_c) * step_p[c]
        dx_parts = []
        d_score = d_s[g]
        for pair in range(HPC // 2):
            ln = slice(pair * 128, pair * 128 + 128)
            x_pair = x_low[:, ln]
            dy_pair = dy[:, ln]
            dy_low = dy_pair.astype(BF16)
            zero = jnp.zeros((T, 128), F32)
            ds = []
            for q in range(2):
                h = c * HPC + pair * 2 + q
                own = jnp.where(half, dy_pair, zero) if q == 0 else jnp.where(half, zero, dy_pair)
                d_mix = dot(own.astype(BF16), x_pair, ca=1, cb=1).astype(BF16).astype(F32)
                d_score = d_score + d_mix * weight[h]
                ds.append(dot(mix[h], dy_low, ca=0, cb=0))
            dx_parts.append(jnp.where(half, ds[0], ds[1]))
        d_s[g] = d_score
        dx1 = jnp.concatenate(dx_parts, axis=1)
        skip = expand(c)
        both = dx1 + d_w
        q2 = x_f * both
        q1 = dy * (total - skip * x_f) - q2
        sel = selector(c)
        sel_low = sel.astype(BF16)
        acc1[...] += split_dot(q1, sel_low)
        acc2[...] += split_dot(q2, sel_low)
        last_row = jnp.sum(d_w * x_f, axis=0, keepdims=True) + decay * jnp.sum(
            after_f * held.astype(F32), axis=0, keepdims=True
        )
        skip_row = jnp.sum(dy * x_f, axis=0, keepdims=True)
        which = lax.broadcasted_iota(jnp.int32, (8, CHUNK), 0)
        two = jnp.where(which == 0, last_row, jnp.where(which == 1, skip_row, 0.0))
        acc_row[...] += dot(two, sel, precision=HIGH)

        d_x = (both + skip * dy).astype(BF16).astype(F32)
        d_pre = d_x * silu_slope(pre_x[:, at])
        tap[0:8, :] = halo_x[:, at].astype(F32)[8:16]
        tap[8 : 8 + T, :] = x_ref[:, at].astype(F32)
        full, taps = conv_back(CHUNK, d_pre, wx_ref[:, at])
        for k in range(CONV):
            part[k : k + 1, at] = taps[k]
        border_send[:, at] = full[0:8]
        gx_ref[:, at] = full[8:].astype(BF16)
        tail_x[:, at] = full[T - 8 :]
        return carry

    lax.fori_loop(0, chunks, gate_back, 0)

    for g in range(groups):
        d_low = d_s[g].astype(BF16)
        d_c[g] += dot(d_low, bcc[0, g])
        d_b[g] += dot(d_low, bcc[1, g], ca=0, cb=0)
    for kind in range(2):
        for g in range(groups):
            at = slice(g * STATE, (g + 1) * STATE)
            out_at = slice(kind * columns + g * STATE, kind * columns + (g + 1) * STATE)
            grad = (d_b if kind == 0 else d_c)[g].astype(BF16).astype(F32)
            d_pre = grad * silu_slope(pre_bc[kind, g])
            tap[0:8, 0:STATE] = halo_bc[kind, :, at].astype(F32)[8:16]
            tap[8 : 8 + T, 0:STATE] = bc_ref[kind, :, at].astype(F32)
            full, taps = conv_back(STATE, d_pre, wbc_ref[kind, :, at])
            for k in range(CONV):
                part[8 + k : 9 + k, out_at] = taps[k]
            border_send[:, width + kind * columns + g * STATE : width + kind * columns + (g + 1) * STATE] = full[0:8]
            gbc_ref[kind, :, at] = full[8:].astype(BF16)
            tail_bc[kind, :, at] = full[T - 8 :]

    border = remote(border_send, border_recv, bo_s.at[0], bo_r.at[0], ctx=prv)

    @pl.when(me > 0)
    def _():
        border.start()

    is_last = lax.broadcasted_iota(jnp.int32, (T, heads), 0) == T - 1
    d_cum = acc1[...] + jnp.where(is_last, acc_row[0:1, :], 0.0)
    d_log = dot(lower, d_cum, ca=0, cb=0, precision=HIGH)
    shifted = logits_ref[...] + params_ref[0:1, :]
    step = jnp.maximum(shifted, 0.0) + jnp.log1p(jnp.exp(-jnp.abs(shifted)))
    rate = -jnp.exp(params_ref[1:2, :])
    d_step = acc2[...] / step + d_log * rate
    d_logit = d_step * sigmoid(shifted)
    gstep_ref[...] = d_logit
    part[12:13, 0:heads] = jnp.sum(d_logit, axis=0, keepdims=True)
    part[13:14, 0:heads] = jnp.sum(d_log * step, axis=0, keepdims=True) * rate
    part[14:15, 0:heads] = acc_row[1:2, :]

    totals[me] = part[...].astype(BF16)

    def total_copy(k):
        return remote(
            totals.at[me], totals.at[me], to_s.at[k], to_r.at[k], ctx=lax.rem(me + k, n_ctx)
        )

    for k in range(1, n_ctx):
        total_copy(k).start()

    @pl.when(me < n_ctx - 1)
    def _():
        border.wait_recv()
        pad = jnp.zeros((8, width), F32)
        gx_ref[T - 16 : T, :] = (
            tail_x[...] + jnp.concatenate([pad, border_recv[:, 0:width]], axis=0)
        ).astype(BF16)
        for kind in range(2):
            pad2 = jnp.zeros((8, columns), F32)
            got = border_recv[:, width + kind * columns : width + (kind + 1) * columns]
            gbc_ref[kind, T - 16 : T, :] = (
                tail_bc[kind] + jnp.concatenate([pad2, got], axis=0)
            ).astype(BF16)

    for k in range(1, n_ctx):
        source = lax.rem(me + n_ctx - k, n_ctx)
        remote(totals.at[source], totals.at[source], to_s.at[k], to_r.at[k], ctx=source).wait_recv()
    whole = totals[0].astype(F32)
    for k in range(1, n_ctx):
        whole = whole + totals[k].astype(F32)
    gwx_ref[...] = whole[0:4]
    ggain_ref[...] = whole[4:5]
    for kind in range(2):
        gwbc_ref[kind] = whole[8:12, kind * columns : (kind + 1) * columns]
    gparams_ref[...] = whole[12:15, 0:heads]

    for k in range(1, n_ctx):
        total_copy(k).wait_send()

    @pl.when(me > 0)
    def _():
        border.wait_send()

    def drain(c, carry):
        @pl.when(me < n_ctx - 1)
        def _():
            forward_copy(c).wait_send()

        @pl.when(me > 0)
        def _():
            reverse_copy(c).wait_send()

        return carry

    lax.fori_loop(0, chunks, drain, 0)


def shards(n_ctx, n_head, x, bc, gate, logits, wx, wbc, params, gain, go):
    T, width = x.shape
    columns = bc.shape[2]
    groups = columns // STATE
    heads = width // HEAD_DIM
    chunks = width // CHUNK
    V = pltpu.VMEM
    D = pltpu.SemaphoreType.DMA
    out_shape = (
        jax.ShapeDtypeStruct(x.shape, BF16),
        jax.ShapeDtypeStruct(bc.shape, BF16),
        jax.ShapeDtypeStruct(x.shape, BF16),
        jax.ShapeDtypeStruct(logits.shape, F32),
        jax.ShapeDtypeStruct(wx.shape, F32),
        jax.ShapeDtypeStruct(wbc.shape, F32),
        jax.ShapeDtypeStruct(params.shape, F32),
        jax.ShapeDtypeStruct((1, width), F32),
    )
    scratch = [
        V((16, width), BF16), V((2, 16, columns), BF16),
        V((heads, T, 128), F32), V((chunks, T, CHUNK), F32), V((chunks, T, CHUNK), F32),
        V((heads, T), F32), V((heads, T), F32), V((T, T), F32),
        V((T + 8, CHUNK), F32), V((T + 16, CHUNK), F32),
        V((T, width), BF16), V((T, width), F32),
        V((2, groups, T, STATE), BF16), V((2, groups, T, STATE), F32),
        V((groups, STATE, T), BF16), V((groups, STATE, T), BF16), V((groups, T, T), F32),
        V((heads, T, T), BF16), V((heads, T, T), F32),
        V((T, width), BF16), V((STATE, width), F32),
        V((chunks, STATE, CHUNK), BF16), V((chunks, STATE, CHUNK), BF16),
        V((chunks, STATE, CHUNK), BF16), V((chunks, STATE, CHUNK), BF16),
        V((T, width), F32), V((T, width), F32),
        V((T, CHUNK), F32), V((T, CHUNK), F32), V((n_head, 16, T), F32),
        V((groups, T, STATE), F32), V((groups, T, STATE), F32), V((groups, T, T), F32),
        V((T, heads), F32), V((T, heads), F32), V((8, heads), F32),
        V((8, width + 2 * columns), F32), V((8, width + 2 * columns), F32),
        V((16, width), F32), V((2, 16, columns), F32),
        V((16, width), F32), V((n_ctx, 16, width), BF16),
        D((2,)), D((2,)),
        D((chunks,)), D((chunks,)), D((chunks,)), D((chunks,)),
        D((n_head,)), D((n_head,)), D((1,)), D((1,)), D((n_ctx,)), D((n_ctx,)),
    ]
    outs = pl.pallas_call(
        functools.partial(kernel, n_ctx, n_head),
        out_shape=out_shape,
        in_specs=[pl.BlockSpec(memory_space=pltpu.VMEM)] * 9,
        out_specs=tuple([pl.BlockSpec(memory_space=pltpu.VMEM)] * 8),
        scratch_shapes=scratch,
        compiler_params=pltpu.CompilerParams(
            collective_id=0, has_side_effects=True, vmem_limit_bytes=60 * 1024 * 1024
        ),
        name="mixer_step",
    )(x, bc, gate, logits, wx, wbc, params, gain.reshape(1, width), go)
    return outs[:7] + (outs[7].reshape(width),)


def solution(mesh):
    return jax.shard_map(
        functools.partial(shards, mesh.shape["ctx"], mesh.shape["head"]),
        mesh=mesh,
        in_specs=(
            P(("group", "ctx"), "head"),
            P(None, ("group", "ctx"), "head"),
            P(("group", "ctx"), "head"),
            P(("group", "ctx"), "head"),
            P(None, "head"),
            P(None, None, "head"),
            P(None, "head"),
            P("head"),
            P(("group", "ctx"), "head"),
        ),
        out_specs=(
            P(("group", "ctx"), "head"),
            P(None, ("group", "ctx"), "head"),
            P(("group", "ctx"), "head"),
            P(("group", "ctx"), "head"),
            P("group", "head"),
            P("group", None, "head"),
            P("group", "head"),
            P(("group", "head")),
        ),
        check_vma=False,
    )
```
